32 devices in a mesh: dp: 8 (over z, y), mp: 4 (over x, core).
Axes of the slice: x: 2, y: 2, z: 4, core: 2. Of those that a mesh axis runs over, the one named last changes fastest.
Arguments:
- activations: bfloat16 [4, 4096, 5120], P(None, 'dp'), may hold values from -60 to 60
- task_weights: bfloat16 [4, 5120, 512], P(None, 'dp', 'mp'), may hold values from -6 to 6
Outputs:
- merged: float32 [5120, 512], P('dp', 'mp')
The draws below stay inside these ranges and needn't reach their ends.
All inputs are finite; a program needn't handle non-finite values.
Results may differ from the reference program's by a relative error of at most 0.0015.
Values may be sent and summed in bfloat16 or wider, within the bound.
A program may use at most 128 MiB of HBM per device.

```python
import math
import jax
import jax.numpy as jnp
from jax import lax

D = 5120
TASKS = 4
ITERS = 2
TOK_TASK = 4096
SLAB = 512


def draw_activations(key, part):
    key_feat = jax.random.fold_in(key, 11)
    key_tok = jax.random.fold_in(key, 12)
    key_base = jax.random.fold_in(key, 13)
    feature_scale = jnp.exp(jax.random.uniform(key_feat, (TASKS, 1, D), jnp.float32, 0.0, math.log(10.0)))
    token_scale = jnp.exp(jax.random.uniform(key_tok, (TASKS, TOK_TASK, 1), jnp.float32, 0.0, math.log(3.0)))
    base = jnp.clip(jax.random.normal(key_base, (TASKS, TOK_TASK, D), jnp.float32), -6.0, 6.0)
    return (base * feature_scale * token_scale / 3.0).astype(jnp.bfloat16)


def level_of(key, extent, cuts, least, top_value):
    factor_of = 1.0
    for axis_at, blocks in cuts:
        steps = jax.random.uniform(jax.random.fold_in(jax.random.fold_in(key, 6), axis_at), (blocks,), jnp.float32, least / len(cuts), top_value / len(cuts))
        factor_of = factor_of * jnp.repeat(jnp.exp(steps), extent[axis_at] // blocks).reshape((-1,) + (1,) * (len(extent) - 1 - axis_at))
    return factor_of


def gaussian(own_key, shape, deviation, reach, split=(), dtype=jnp.bfloat16):
    array = deviation * jax.random.normal(own_key, shape, jnp.float32)
    if split:
        array = array * level_of(own_key, shape, split, -0.22, 0.18)
    return jnp.clip(array, -reach, reach).astype(dtype)


def setup_inputs(seed: int = 0) -> dict:
    key_of = jax.random.split(jax.random.key(seed), 3)
    activations = draw_activations(jax.random.fold_in(key_of[2], 71), 0)
    task_weights = gaussian(key_of[1], (TASKS, D, SLAB), 1.0, 6.0, ((1, 8), (2, 4)))
    return dict(activations=activations, task_weights=task_weights)


ALPHA = 0.9


def reference(activations, task_weights):
    total = TASKS * TOK_TASK
    flat = activations.reshape(-1, D)
    gram = jnp.dot(flat.T, flat, preferred_element_type=jnp.float32) / total
    row_ids = lax.broadcasted_iota(jnp.int32, (D, D), 0)
    col_ids = lax.broadcasted_iota(jnp.int32, (D, D), 1)
    operator = jnp.where(row_ids == col_ids, gram, ALPHA * gram)
    cross = jnp.zeros((D, SLAB), jnp.float32)
    diag_part = jnp.zeros((D, SLAB), jnp.float32)
    for task in range(TASKS):
        outputs = jnp.dot(activations[task], task_weights[task], preferred_element_type=jnp.float32).astype(jnp.bfloat16)
        cross = cross + jnp.dot(activations[task].T, outputs, preferred_element_type=jnp.float32)
        squares = jnp.sum(activations[task].astype(jnp.float32) ** 2, axis=0)
        diag_part = diag_part + squares[:, None] * task_weights[task].astype(jnp.float32)
    target = (ALPHA * cross + (1.0 - ALPHA) * diag_part) / total

    def apply(vector):
        return jnp.dot(operator, vector, precision=lax.Precision.HIGHEST)

    merged = jnp.mean(task_weights.astype(jnp.float32), axis=0)
    residual = target - apply(merged)
    direction = residual
    norm_now = jnp.sum(residual * residual, axis=0)
    for step in range(ITERS):
        image = apply(direction)
        alpha = norm_now / jnp.sum(direction * image, axis=0)
        merged = merged + alpha * direction
        if step + 1 < ITERS:
            residual = residual - alpha * image
            norm_next = jnp.sum(residual * residual, axis=0)
            direction = residual + (norm_next / norm_now) * direction
            norm_now = norm_next
    return merged
```

```python
import jax
import jax.numpy as jnp
from jax import lax
from jax.sharding import PartitionSpec as P

ALPHA = 0.9


def dot(left, right, dims):
    return lax.dot_general(
        left, right, (dims, ((), ())), preferred_element_type=jnp.float32
    )


def rounded(array):
    return lax.reduce_precision(array, 8, 7)


def split_pair(array):
    coarse = rounded(array)
    high = coarse.astype(jnp.bfloat16)
    low = (array - coarse).astype(jnp.bfloat16)
    return jnp.concatenate([high, low], axis=1)


def shards(activations, task_weights):
    tasks, tokens, width = activations.shape
    cols = task_weights.shape[2]
    total = tasks * tokens * lax.axis_size("dp")
    bf16, f32 = jnp.bfloat16, jnp.float32
    flat = activations.reshape(tasks * tokens, width)
    weights = lax.all_gather(task_weights, "dp", axis=1, tiled=True)
    squares = jnp.sum(jnp.square(activations.astype(f32)), axis=1)
    squares_all = jnp.sum(squares, axis=0)[:, None]
    mean = jnp.mean(weights.astype(f32), axis=0)
    mean_pair = split_pair(mean)
    gaps = []
    for task in range(tasks):
        wide = dot(
            activations[task],
            jnp.concatenate([weights[task], mean_pair], axis=1),
            ((1,), (0,)),
        )
        outputs = rounded(wide[:, :cols])
        gaps.append(outputs - (wide[:, cols : 2 * cols] + wide[:, 2 * cols :]))
    gap = split_pair(jnp.concatenate(gaps, axis=0))
    diag = sum(
        squares[t][:, None] * (weights[t].astype(f32) - mean) for t in range(tasks)
    )
    inner = dot(flat, gap, ((0,), (0,)))
    inner = inner[:, :cols] + inner[:, cols:]
    residual = lax.psum_scatter(
        (ALPHA * inner + (1.0 - ALPHA) * diag) / total,
        "dp",
        scatter_dimension=0,
        tiled=True,
    )
    full_bf = lax.all_gather(residual.astype(bf16), "dp", axis=0, tiled=True)
    full = full_bf.astype(f32)
    projected = split_pair(dot(flat, full_bf, ((1,), (0,))))
    inner = dot(flat, projected, ((0,), (0,)))
    inner = inner[:, :cols] + inner[:, cols:]
    image = lax.psum_scatter(
        (ALPHA * inner + (1.0 - ALPHA) * squares_all * full) / total,
        "dp",
        scatter_dimension=0,
        tiled=True,
    )
    image_full = lax.all_gather(image.astype(bf16), "dp", axis=0, tiled=True).astype(f32)
    norm0 = jnp.sum(full * full, axis=0)
    alpha0 = norm0 / jnp.sum(full * image_full, axis=0)
    next_full = full - alpha0 * image_full
    norm1 = jnp.sum(next_full * next_full, axis=0)
    beta = norm1 / norm0
    direction = next_full + beta * full
    direction_bf = direction.astype(bf16)
    direction = direction_bf.astype(f32)
    projected = dot(flat, direction_bf, ((1,), (0,)))
    energy = lax.psum(
        (
            ALPHA * jnp.sum(projected * projected, axis=0)
            + (1.0 - ALPHA) * jnp.sum(squares_all * direction * direction, axis=0)
        )
        / total,
        "dp",
    )
    alpha1 = norm1 / energy
    own_mean = jnp.mean(task_weights.astype(f32), axis=0)
    return (
        own_mean
        + alpha0 * residual
        + alpha1 * (residual - alpha0 * image + beta * residual)
    )


def solution(mesh):
    return jax.shard_map(
        shards,
        mesh=mesh,
        in_specs=(P(None, "dp", None), P(None, "dp", "mp")),
        out_specs=P("dp", "mp"),
        check_vma=False,
    )
```

```python
import functools

import jax
import jax.numpy as jnp
from jax import lax
from jax.experimental import pallas as pl
from jax.experimental.pallas import tpu as pltpu
from jax.sharding import PartitionSpec as P

ALPHA = 0.9


MESH = pl.DeviceIdType.MESH


def inner_of(count):
    inner = 1
    for size in range(1, count + 1):
        if count % size == 0 and size * size <= count:
            inner = size
    return inner


def remote(source, target, send, receive, device):
    return pltpu.make_async_remote_copy(
        src_ref=source,
        dst_ref=target,
        send_sem=send,
        recv_sem=receive,
        device_id={"dp": device},
        device_id_type=MESH,
    )


def greet(devices):
    barrier = pltpu.get_barrier_semaphore()
    for device in devices:
        pl.semaphore_signal(
            barrier, inc=1, device_id={"dp": device}, device_id_type=MESH
        )
    pl.semaphore_wait(barrier, len(devices))


def places(count, inner):
    outer = count // inner
    me = lax.axis_index("dp")
    mine_out, mine_in = me // inner, me % inner
    near = [mine_out * inner + (mine_in + d) % inner for d in range(1, inner)]
    far = [((mine_out + r) % outer) * inner + mine_in for r in range(1, outer)]
    behind = [
        ((mine_out - r + outer) % outer) * inner + mine_in for r in range(1, outer)
    ]
    return me, mine_out, mine_in, near, far, behind


def reduce_gather_kernel(
    count,
    inner,
    part_ref,
    own_ref,
    full_ref,
    stage,
    near_in,
    sums,
    far_in,
    near_send,
    near_recv,
    far_send,
    far_recv,
    out_send,
    out_recv,
    spread_send,
    spread_recv,
):
    outer = count // inner
    me, mine_out, mine_in, near, far, behind = places(count, inner)
    rows = own_ref.shape[0]
    f32 = jnp.float32

    def block(index):
        return pl.ds(pl.multiple_of(index * rows, rows), rows)

    greet(near + far)
    order = list(range(1, outer)) + [0]
    copies = {}
    for r in order:
        base = ((mine_out + r) % outer) * inner
        for d in range(1, inner):
            stage[r, d - 1] = part_ref[block(base + (mine_in + d) % inner)].astype(
                stage.dtype
            )
            copies[r, d] = remote(
                stage.at[r, d - 1],
                near_in.at[r, d - 1],
                near_send.at[r, d - 1],
                near_recv.at[r, d - 1],
                near[d - 1],
            )
            copies[r, d].start()
    hops = []
    for r in order:
        base = ((mine_out + r) % outer) * inner
        value = part_ref[block(base + mine_in)]
        for d in range(1, inner):
            copies[r, d].wait_recv()
            value = value + near_in[r, d - 1].astype(f32)
        if r:
            sums[r - 1] = value.astype(sums.dtype)
            hop = remote(
                sums.at[r - 1],
                far_in.at[r - 1],
                far_send.at[r - 1],
                far_recv.at[r - 1],
                far[r - 1],
            )
            hop.start()
            hops.append(hop)
        else:
            own_ref[...] = value
    value = own_ref[...]
    for r in range(1, outer):
        hops[r - 1].wait_recv()
        value = value + far_in[r - 1].astype(f32)
    own_ref[...] = value
    full_ref[block(me)] = value.astype(full_ref.dtype)

    def spread(slot, index):
        made = []
        for d in range(1, inner):
            copy = remote(
                full_ref.at[block(index)],
                full_ref.at[block(index)],
                spread_send.at[slot, d - 1],
                spread_recv.at[slot, d - 1],
                near[d - 1],
            )
            copy.start()
            made.append(copy)
        return made

    outs = []
    for r in range(1, outer):
        copy = remote(
            full_ref.at[block(me)],
            full_ref.at[block(me)],
            out_send.at[r - 1],
            out_recv.at[r - 1],
            far[r - 1],
        )
        copy.start()
        outs.append(copy)
    spreads = spread(0, me)
    for r in range(1, outer):
        outs[r - 1].wait_recv()
        spreads += spread(r, behind[r - 1])
    for copy in spreads:
        copy.wait_recv()
    for copy in list(copies.values()) + hops + outs + spreads:
        copy.wait_send()


def reduce_gather(part, wire, collective_id):
    count = lax.axis_size("dp")
    inner = inner_of(count)
    outer = count // inner
    rows, cols = part.shape[0] // count, part.shape[1]
    near, far = max(inner - 1, 1), max(outer - 1, 1)
    dma = pltpu.SemaphoreType.DMA
    vmem = pl.BlockSpec(memory_space=pltpu.VMEM)
    return pl.pallas_call(
        functools.partial(reduce_gather_kernel, count, inner),
        out_shape=(
            jax.ShapeDtypeStruct((rows, cols), jnp.float32),
            jax.ShapeDtypeStruct((count * rows, cols), jnp.bfloat16),
        ),
        in_specs=[vmem],
        out_specs=(vmem, vmem),
        scratch_shapes=[
            pltpu.VMEM((outer, near, rows, cols), wire),
            pltpu.VMEM((outer, near, rows, cols), wire),
            pltpu.VMEM((far, rows, cols), wire),
            pltpu.VMEM((far, rows, cols), wire),
            dma((outer, near)),
            dma((outer, near)),
            dma((far,)),
            dma((far,)),
            dma((far,)),
            dma((far,)),
            dma((outer, near)),
            dma((outer, near)),
        ],
        compiler_params=pltpu.CompilerParams(
            collective_id=collective_id, has_side_effects=True
        ),
    )(part)


def total_kernel(count, in_ref, out_ref, slots, send, receive):
    me = lax.axis_index("dp")
    others = [(me + d) % count for d in range(1, count)]
    greet(others)
    copies = []
    for d, device in enumerate(others):
        copy = remote(in_ref, slots.at[d], send.at[d], receive.at[d], device)
        copy.start()
        copies.append(copy)
    value = in_ref[...]
    for d, copy in enumerate(copies):
        copy.wait_recv()
        value = value + slots[d]
    out_ref[...] = value
    for copy in copies:
        copy.wait_send()


def total_over(part, collective_id):
    count = lax.axis_size("dp")
    dma = pltpu.SemaphoreType.DMA
    vmem = pl.BlockSpec(memory_space=pltpu.VMEM)
    return pl.pallas_call(
        functools.partial(total_kernel, count),
        out_shape=jax.ShapeDtypeStruct(part.shape, jnp.float32),
        in_specs=[vmem],
        out_specs=vmem,
        scratch_shapes=[
            pltpu.VMEM((count - 1,) + part.shape, jnp.float32),
            dma((count - 1,)),
            dma((count - 1,)),
        ],
        compiler_params=pltpu.CompilerParams(
            collective_id=collective_id, has_side_effects=True
        ),
    )(part)


def dot(left, right, dims):
    return lax.dot_general(
        left, right, (dims, ((), ())), preferred_element_type=jnp.float32
    )


def rounded(array):
    return lax.reduce_precision(array, 8, 7)


def split_pair(array):
    coarse = rounded(array)
    high = coarse.astype(jnp.bfloat16)
    low = (array - coarse).astype(jnp.bfloat16)
    return jnp.concatenate([high, low], axis=1)


def shards(activations, task_weights):
    tasks, tokens, width = activations.shape
    cols = task_weights.shape[2]
    total = tasks * tokens * lax.axis_size("dp")
    bf16, f32 = jnp.bfloat16, jnp.float32
    flat = activations.reshape(tasks * tokens, width)
    weights = lax.all_gather(task_weights, "dp", axis=1, tiled=True)
    squares = jnp.sum(jnp.square(activations.astype(f32)), axis=1)
    squares_all = jnp.sum(squares, axis=0)[:, None]
    mean = jnp.mean(weights.astype(f32), axis=0)
    mean_pair = split_pair(mean)
    gaps = []
    for task in range(tasks):
        wide = dot(
            activations[task],
            jnp.concatenate([weights[task], mean_pair], axis=1),
            ((1,), (0,)),
        )
        outputs = rounded(wide[:, :cols])
        gaps.append(outputs - (wide[:, cols : 2 * cols] + wide[:, 2 * cols :]))
    gap = split_pair(jnp.concatenate(gaps, axis=0))
    diag = sum(
        squares[t][:, None] * (weights[t].astype(f32) - mean) for t in range(tasks)
    )
    inner = dot(flat, gap, ((0,), (0,)))
    inner = inner[:, :cols] + inner[:, cols:]
    residual, full_bf = reduce_gather(
        (ALPHA * inner + (1.0 - ALPHA) * diag) / total, f32, 1
    )
    full = full_bf.astype(f32)
    projected = split_pair(dot(flat, full_bf, ((1,), (0,))))
    inner = dot(flat, projected, ((0,), (0,)))
    inner = inner[:, :cols] + inner[:, cols:]
    image, image_bf = reduce_gather(
        (ALPHA * inner + (1.0 - ALPHA) * squares_all * full) / total, bf16, 2
    )
    image_full = image_bf.astype(f32)
    norm0 = jnp.sum(full * full, axis=0)
    alpha0 = norm0 / jnp.sum(full * image_full, axis=0)
    next_full = full - alpha0 * image_full
    norm1 = jnp.sum(next_full * next_full, axis=0)
    beta = norm1 / norm0
    direction = next_full + beta * full
    direction_bf = direction.astype(bf16)
    direction = direction_bf.astype(f32)
    projected = dot(flat, direction_bf, ((1,), (0,)))
    energy = (
        ALPHA * jnp.sum(projected * projected, axis=0)
        + (1.0 - ALPHA) * jnp.sum(squares_all * direction * direction, axis=0)
    ) / total
    energy = total_over(jnp.broadcast_to(energy, (8, cols)), 3)[0]
    alpha1 = norm1 / energy
    own_mean = jnp.mean(task_weights.astype(f32), axis=0)
    return (
        own_mean
        + alpha0 * residual
        + alpha1 * (residual - alpha0 * image + beta * residual)
    )


def solution(mesh):
    return jax.shard_map(
        shards,
        mesh=mesh,
        in_specs=(P(None, "dp", None), P(None, "dp", "mp")),
        out_specs=P("dp", "mp"),
        check_vma=False,
    )
```

```python
import functools

import jax
import jax.numpy as jnp
from jax import lax
from jax.experimental import pallas as pl
from jax.experimental.pallas import tpu as pltpu
from jax.sharding import PartitionSpec as P

ALPHA = 0.9


MESH = pl.DeviceIdType.MESH


def inner_of(count):
    inner = 1
    for size in range(1, count + 1):
        if count % size == 0 and size * size <= count:
            inner = size
    return inner


def remote(source, target, send, receive, device):
    return pltpu.make_async_remote_copy(
        src_ref=source,
        dst_ref=target,
        send_sem=send,
        recv_sem=receive,
        device_id={"dp": device},
        device_id_type=MESH,
    )


def greet(devices):
    barrier = pltpu.get_barrier_semaphore()
    for device in devices:
        pl.semaphore_signal(
            barrier, inc=1, device_id={"dp": device}, device_id_type=MESH
        )
    pl.semaphore_wait(barrier, len(devices))


def places(count, inner):
    outer = count // inner
    me = lax.axis_index("dp")
    mine_out, mine_in = me // inner, me % inner
    near = [mine_out * inner + (mine_in + d) % inner for d in range(1, inner)]
    far = [((mine_out + r) % outer) * inner + mine_in for r in range(1, outer)]
    behind = [
        ((mine_out - r + outer) % outer) * inner + mine_in for r in range(1, outer)
    ]
    return me, mine_out, mine_in, near, far, behind


def reduce_gather_kernel(
    count,
    inner,
    part_ref,
    own_ref,
    full_ref,
    stage,
    near_in,
    sums,
    far_in,
    near_send,
    near_recv,
    far_send,
    far_recv,
    out_send,
    out_recv,
    spread_send,
    spread_recv,
):
    outer = count // inner
    me, mine_out, mine_in, near, far, behind = places(count, inner)
    rows = own_ref.shape[0]
    f32 = jnp.float32

    def block(index):
        return pl.ds(pl.multiple_of(index * rows, rows), rows)

    greet(near + far)
    order = list(range(1, outer)) + [0]
    copies = {}
    for r in order:
        base = ((mine_out + r) % outer) * inner
        for d in range(1, inner):
            stage[r, d - 1] = part_ref[block(base + (mine_in + d) % inner)].astype(
                stage.dtype
            )
            copies[r, d] = remote(
                stage.at[r, d - 1],
                near_in.at[r, d - 1],
                near_send.at[r, d - 1],
                near_recv.at[r, d - 1],
                near[d - 1],
            )
            copies[r, d].start()
    hops = []
    for r in order:
        base = ((mine_out + r) % outer) * inner
        value = part_ref[block(base + mine_in)]
        for d in range(1, inner):
            copies[r, d].wait_recv()
            value = value + near_in[r, d - 1].astype(f32)
        if r:
            sums[r - 1] = value.astype(sums.dtype)
            hop = remote(
                sums.at[r - 1],
                far_in.at[r - 1],
                far_send.at[r - 1],
                far_recv.at[r - 1],
                far[r - 1],
            )
            hop.start()
            hops.append(hop)
        else:
            own_ref[...] = value
    value = own_ref[...]
    for r in range(1, outer):
        hops[r - 1].wait_recv()
        value = value + far_in[r - 1].astype(f32)
    own_ref[...] = value
    full_ref[block(me)] = value.astype(full_ref.dtype)

    def spread(slot, index):
        made = []
        for d in range(1, inner):
            copy = remote(
                full_ref.at[block(index)],
                full_ref.at[block(index)],
                spread_send.at[slot, d - 1],
                spread_recv.at[slot, d - 1],
                near[d - 1],
            )
            copy.start()
            made.append(copy)
        return made

    outs = []
    for r in range(1, outer):
        copy = remote(
            full_ref.at[block(me)],
            full_ref.at[block(me)],
            out_send.at[r - 1],
            out_recv.at[r - 1],
            far[r - 1],
        )
        copy.start()
        outs.append(copy)
    spreads = spread(0, me)
    for r in range(1, outer):
        outs[r - 1].wait_recv()
        spreads += spread(r, behind[r - 1])
    for copy in spreads:
        copy.wait_recv()
    for copy in list(copies.values()) + hops + outs + spreads:
        copy.wait_send()


def reduce_gather(part, wire, collective_id):
    count = lax.axis_size("dp")
    inner = inner_of(count)
    outer = count // inner
    rows, cols = part.shape[0] // count, part.shape[1]
    near, far = max(inner - 1, 1), max(outer - 1, 1)
    dma = pltpu.SemaphoreType.DMA
    vmem = pl.BlockSpec(memory_space=pltpu.VMEM)
    return pl.pallas_call(
        functools.partial(reduce_gather_kernel, count, inner),
        out_shape=(
            jax.ShapeDtypeStruct((rows, cols), jnp.float32),
            jax.ShapeDtypeStruct((count * rows, cols), jnp.bfloat16),
        ),
        in_specs=[vmem],
        out_specs=(vmem, vmem),
        scratch_shapes=[
            pltpu.VMEM((outer, near, rows, cols), wire),
            pltpu.VMEM((outer, near, rows, cols), wire),
            pltpu.VMEM((far, rows, cols), wire),
            pltpu.VMEM((far, rows, cols), wire),
            dma((outer, near)),
            dma((outer, near)),
            dma((far,)),
            dma((far,)),
            dma((far,)),
            dma((far,)),
            dma((outer, near)),
            dma((outer, near)),
        ],
        compiler_params=pltpu.CompilerParams(
            collective_id=collective_id, has_side_effects=True
        ),
    )(part)


def gather_kernel(
    count,
    inner,
    wide,
    in_ref,
    x_ref,
    full_ref,
    squares_ref,
    held,
    load,
    out_send,
    out_recv,
    spread_send,
    spread_recv,
):
    outer = count // inner
    me, mine_out, mine_in, near, far, behind = places(count, inner)
    tasks, rows, _ = in_ref.shape
    width = x_ref.shape[2]

    def block(index):
        return pl.ds(pl.multiple_of(index * rows, rows), rows)

    def fetch(task):
        return pltpu.make_async_copy(
            x_ref.at[task], held.at[task % 2], load.at[task % 2]
        )

    fetch(0).start()
    greet(near + far)
    outs, spreads = {}, []
    for task in range(tasks):
        for r in range(1, outer):
            outs[task, r] = remote(
                in_ref.at[task],
                full_ref.at[task, block(me)],
                out_send.at[task, r - 1],
                out_recv.at[task, r - 1],
                far[r - 1],
            )
            outs[task, r].start()
        for d in range(1, inner):
            copy = remote(
                in_ref.at[task],
                full_ref.at[task, block(me)],
                spread_send.at[task, 0, d - 1],
                spread_recv.at[task, 0, d - 1],
                near[d - 1],
            )
            copy.start()
            spreads.append(copy)
    for task in range(tasks):
        full_ref[task, block(me)] = in_ref[task]
    for task in range(tasks):
        fetch(task).wait()
        if task + 1 < tasks:
            fetch(task + 1).start()

        def body(step, carry, task=task):
            span = pl.ds(pl.multiple_of(step * wide, wide), wide)
            value = held[task % 2, :, span].astype(jnp.float32)
            squares_ref[task, :, span] = jnp.sum(
                value * value, axis=0, keepdims=True
            )
            return carry

        lax.fori_loop(0, width // wide, body, 0)
    for task in range(tasks):
        for r in range(1, outer):
            outs[task, r].wait_recv()
            for d in range(1, inner):
                copy = remote(
                    full_ref.at[task, block(behind[r - 1])],
                    full_ref.at[task, block(behind[r - 1])],
                    spread_send.at[task, r, d - 1],
                    spread_recv.at[task, r, d - 1],
                    near[d - 1],
                )
                copy.start()
                spreads.append(copy)
    for copy in spreads:
        copy.wait_recv()
    for copy in list(outs.values()) + spreads:
        copy.wait_send()


def gather_weights(task_weights, activations, collective_id):
    count = lax.axis_size("dp")
    inner = inner_of(count)
    outer = count // inner
    tasks, rows, cols = task_weights.shape
    _, tokens, width = activations.shape
    near, far = max(inner - 1, 1), max(outer - 1, 1)
    wide = 256 if width % 256 == 0 else width
    dma = pltpu.SemaphoreType.DMA
    vmem = pl.BlockSpec(memory_space=pltpu.VMEM)
    return pl.pallas_call(
        functools.partial(gather_kernel, count, inner, wide),
        out_shape=(
            jax.ShapeDtypeStruct((tasks, count * rows, cols), task_weights.dtype),
            jax.ShapeDtypeStruct((tasks, 1, width), jnp.float32),
        ),
        in_specs=[vmem, pl.BlockSpec(memory_space=pl.ANY)],
        out_specs=(vmem, vmem),
        scratch_shapes=[
            pltpu.VMEM((2, tokens, width), activations.dtype),
            dma((2,)),
            dma((tasks, far)),
            dma((tasks, far)),
            dma((tasks, outer, near)),
            dma((tasks, outer, near)),
        ],
        compiler_params=pltpu.CompilerParams(
            collective_id=collective_id, has_side_effects=True
        ),
    )(task_weights, activations)


def total_kernel(count, in_ref, out_ref, slots, send, receive):
    me = lax.axis_index("dp")
    others = [(me + d) % count for d in range(1, count)]
    greet(others)
    copies = []
    for d, device in enumerate(others):
        copy = remote(in_ref, slots.at[d], send.at[d], receive.at[d], device)
        copy.start()
        copies.append(copy)
    value = in_ref[...]
    for d, copy in enumerate(copies):
        copy.wait_recv()
        value = value + slots[d]
    out_ref[...] = value
    for copy in copies:
        copy.wait_send()


def total_over(part, collective_id):
    count = lax.axis_size("dp")
    dma = pltpu.SemaphoreType.DMA
    vmem = pl.BlockSpec(memory_space=pltpu.VMEM)
    return pl.pallas_call(
        functools.partial(total_kernel, count),
        out_shape=jax.ShapeDtypeStruct(part.shape, jnp.float32),
        in_specs=[vmem],
        out_specs=vmem,
        scratch_shapes=[
            pltpu.VMEM((count - 1,) + part.shape, jnp.float32),
            dma((count - 1,)),
            dma((count - 1,)),
        ],
        compiler_params=pltpu.CompilerParams(
            collective_id=collective_id, has_side_effects=True
        ),
    )(part)


def dot(left, right, dims):
    return lax.dot_general(
        left, right, (dims, ((), ())), preferred_element_type=jnp.float32
    )


def rounded(array):
    return lax.reduce_precision(array, 8, 7)


def split_pair(array):
    coarse = rounded(array)
    high = coarse.astype(jnp.bfloat16)
    low = (array - coarse).astype(jnp.bfloat16)
    return jnp.concatenate([high, low], axis=1)


def shards(activations, task_weights):
    tasks, tokens, width = activations.shape
    cols = task_weights.shape[2]
    total = tasks * tokens * lax.axis_size("dp")
    bf16, f32 = jnp.bfloat16, jnp.float32
    flat = activations.reshape(tasks * tokens, width)
    weights, squares = gather_weights(task_weights, activations, 4)
    squares = squares.reshape(tasks, width)
    squares_all = jnp.sum(squares, axis=0)[:, None]
    mean = jnp.mean(weights.astype(f32), axis=0)
    mean_pair = split_pair(mean)
    gaps = []
    for task in range(tasks):
        wide = dot(
            activations[task],
            jnp.concatenate([weights[task], mean_pair], axis=1),
            ((1,), (0,)),
        )
        outputs = rounded(wide[:, :cols])
        gaps.append(outputs - (wide[:, cols : 2 * cols] + wide[:, 2 * cols :]))
    gap = split_pair(jnp.concatenate(gaps, axis=0))
    diag = sum(
        squares[t][:, None] * (weights[t].astype(f32) - mean) for t in range(tasks)
    )
    inner = dot(flat, gap, ((0,), (0,)))
    inner = inner[:, :cols] + inner[:, cols:]
    residual, full_bf = reduce_gather(
        (ALPHA * inner + (1.0 - ALPHA) * diag) / total, f32, 1
    )
    full = full_bf.astype(f32)
    projected = split_pair(dot(flat, full_bf, ((1,), (0,))))
    inner = dot(flat, projected, ((0,), (0,)))
    inner = inner[:, :cols] + inner[:, cols:]
    image, image_bf = reduce_gather(
        (ALPHA * inner + (1.0 - ALPHA) * squares_all * full) / total, bf16, 2
    )
    image_full = image_bf.astype(f32)
    norm0 = jnp.sum(full * full, axis=0)
    alpha0 = norm0 / jnp.sum(full * image_full, axis=0)
    next_full = full - alpha0 * image_full
    norm1 = jnp.sum(next_full * next_full, axis=0)
    beta = norm1 / norm0
    direction = next_full + beta * full
    direction_bf = direction.astype(bf16)
    direction = direction_bf.astype(f32)
    projected = dot(flat, direction_bf, ((1,), (0,)))
    energy = (
        ALPHA * jnp.sum(projected * projected, axis=0)
        + (1.0 - ALPHA) * jnp.sum(squares_all * direction * direction, axis=0)
    ) / total
    energy = total_over(jnp.broadcast_to(energy, (8, cols)), 3)[0]
    alpha1 = norm1 / energy
    own_mean = jnp.mean(task_weights.astype(f32), axis=0)
    return (
        own_mean
        + alpha0 * residual
        + alpha1 * (residual - alpha0 * image + beta * residual)
    )


def solution(mesh):
    return jax.shard_map(
        shards,
        mesh=mesh,
        in_specs=(P(None, "dp", None), P(None, "dp", "mp")),
        out_specs=P("dp", "mp"),
        check_vma=False,
    )
```

```python
import functools

import jax
import jax.numpy as jnp
from jax import lax
from jax.experimental import pallas as pl
from jax.experimental.pallas import tpu as pltpu
from jax.sharding import PartitionSpec as P

ALPHA = 0.9


MESH = pl.DeviceIdType.MESH


def inner_of(count):
    inner = 1
    for size in range(1, count + 1):
        if count % size == 0 and size * size <= count:
            inner = size
    return inner


def remote(source, target, send, receive, device):
    return pltpu.make_async_remote_copy(
        src_ref=source,
        dst_ref=target,
        send_sem=send,
        recv_sem=receive,
        device_id={"dp": device},
        device_id_type=MESH,
    )


def greet(devices):
    barrier = pltpu.get_barrier_semaphore()
    for device in devices:
        pl.semaphore_signal(
            barrier, inc=1, device_id={"dp": device}, device_id_type=MESH
        )
    pl.semaphore_wait(barrier, len(devices))


def places(count, inner):
    outer = count // inner
    me = lax.axis_index("dp")
    mine_out, mine_in = me // inner, me % inner
    near = [mine_out * inner + (mine_in + d) % inner for d in range(1, inner)]
    far = [((mine_out + r) % outer) * inner + mine_in for r in range(1, outer)]
    behind = [
        ((mine_out - r + outer) % outer) * inner + mine_in for r in range(1, outer)
    ]
    return me, mine_out, mine_in, near, far, behind


def reduce_gather_kernel(
    count,
    inner,
    part_ref,
    own_ref,
    full_ref,
    stage,
    near_in,
    sums,
    far_in,
    near_send,
    near_recv,
    far_send,
    far_recv,
    out_send,
    out_recv,
    spread_send,
    spread_recv,
):
    outer = count // inner
    me, mine_out, mine_in, near, far, behind = places(count, inner)
    rows = own_ref.shape[0]
    f32 = jnp.float32

    def block(index):
        return pl.ds(pl.multiple_of(index * rows, rows), rows)

    greet(near + far)
    order = list(range(1, outer)) + [0]
    copies = {}
    for r in order:
        base = ((mine_out + r) % outer) * inner
        for d in range(1, inner):
            stage[r, d - 1] = part_ref[block(base + (mine_in + d) % inner)].astype(
                stage.dtype
            )
            copies[r, d] = remote(
                stage.at[r, d - 1],
                near_in.at[r, d - 1],
                near_send.at[r, d - 1],
                near_recv.at[r, d - 1],
                near[d - 1],
            )
            copies[r, d].start()
    hops = []
    for r in order:
        base = ((mine_out + r) % outer) * inner
        value = part_ref[block(base + mine_in)]
        for d in range(1, inner):
            copies[r, d].wait_recv()
            value = value + near_in[r, d - 1].astype(f32)
        if r:
            sums[r - 1] = value.astype(sums.dtype)
            hop = remote(
                sums.at[r - 1],
                far_in.at[r - 1],
                far_send.at[r - 1],
                far_recv.at[r - 1],
                far[r - 1],
            )
            hop.start()
            hops.append(hop)
        else:
            own_ref[...] = value
    value = own_ref[...]
    for r in range(1, outer):
        hops[r - 1].wait_recv()
        value = value + far_in[r - 1].astype(f32)
    own_ref[...] = value
    full_ref[block(me)] = value.astype(full_ref.dtype)

    def spread(slot, index):
        made = []
        for d in range(1, inner):
            copy = remote(
                full_ref.at[block(index)],
                full_ref.at[block(index)],
                spread_send.at[slot, d - 1],
                spread_recv.at[slot, d - 1],
                near[d - 1],
            )
            copy.start()
            made.append(copy)
        return made

    outs = []
    for r in range(1, outer):
        copy = remote(
            full_ref.at[block(me)],
            full_ref.at[block(me)],
            out_send.at[r - 1],
            out_recv.at[r - 1],
            far[r - 1],
        )
        copy.start()
        outs.append(copy)
    spreads = spread(0, me)
    for r in range(1, outer):
        outs[r - 1].wait_recv()
        spreads += spread(r, behind[r - 1])
    for copy in spreads:
        copy.wait_recv()
    for copy in list(copies.values()) + hops + outs + spreads:
        copy.wait_send()


def reduce_gather(part, wire, collective_id):
    count = lax.axis_size("dp")
    inner = inner_of(count)
    outer = count // inner
    rows, cols = part.shape[0] // count, part.shape[1]
    near, far = max(inner - 1, 1), max(outer - 1, 1)
    dma = pltpu.SemaphoreType.DMA
    vmem = pl.BlockSpec(memory_space=pltpu.VMEM)
    return pl.pallas_call(
        functools.partial(reduce_gather_kernel, count, inner),
        out_shape=(
            jax.ShapeDtypeStruct((rows, cols), jnp.float32),
            jax.ShapeDtypeStruct((count * rows, cols), jnp.bfloat16),
        ),
        in_specs=[vmem],
        out_specs=(vmem, vmem),
        scratch_shapes=[
            pltpu.VMEM((outer, near, rows, cols), wire),
            pltpu.VMEM((outer, near, rows, cols), wire),
            pltpu.VMEM((far, rows, cols), wire),
            pltpu.VMEM((far, rows, cols), wire),
            dma((outer, near)),
            dma((outer, near)),
            dma((far,)),
            dma((far,)),
            dma((far,)),
            dma((far,)),
            dma((outer, near)),
            dma((outer, near)),
        ],
        compiler_params=pltpu.CompilerParams(
            collective_id=collective_id, has_side_effects=True
        ),
    )(part)


def gather_kernel(
    count,
    inner,
    wide,
    in_ref,
    x_ref,
    full_ref,
    squares_ref,
    held,
    load,
    out_send,
    out_recv,
    spread_send,
    spread_recv,
):
    outer = count // inner
    me, mine_out, mine_in, near, far, behind = places(count, inner)
    tasks, rows, _ = in_ref.shape
    width = x_ref.shape[2]

    def block(index):
        return pl.ds(pl.multiple_of(index * rows, rows), rows)

    def fetch(task):
        return pltpu.make_async_copy(
            x_ref.at[task], held.at[task % 2], load.at[task % 2]
        )

    fetch(0).start()
    greet(near + far)
    outs, spreads = {}, []
    for task in range(tasks):
        for r in range(1, outer):
            outs[task, r] = remote(
                in_ref.at[task],
                full_ref.at[task, block(me)],
                out_send.at[task, r - 1],
                out_recv.at[task, r - 1],
                far[r - 1],
            )
            outs[task, r].start()
        for d in range(1, inner):
            copy = remote(
                in_ref.at[task],
                full_ref.at[task, block(me)],
                spread_send.at[task, 0, d - 1],
                spread_recv.at[task, 0, d - 1],
                near[d - 1],
            )
            copy.start()
            spreads.append(copy)
    for task in range(tasks):
        full_ref[task, block(me)] = in_ref[task]
    for task in range(tasks):
        fetch(task).wait()
        if task + 1 < tasks:
            fetch(task + 1).start()

        def body(step, carry, task=task):
            span = pl.ds(pl.multiple_of(step * wide, wide), wide)
            value = held[task % 2, :, span].astype(jnp.float32)
            squares_ref[task, :, span] = jnp.sum(
                value * value, axis=0, keepdims=True
            )
            return carry

        lax.fori_loop(0, width // wide, body, 0)
    for task in range(tasks):
        for r in range(1, outer):
            outs[task, r].wait_recv()
            for d in range(1, inner):
                copy = remote(
                    full_ref.at[task, block(behind[r - 1])],
                    full_ref.at[task, block(behind[r - 1])],
                    spread_send.at[task, r, d - 1],
                    spread_recv.at[task, r, d - 1],
                    near[d - 1],
                )
                copy.start()
                spreads.append(copy)
    for copy in spreads:
        copy.wait_recv()
    for copy in list(outs.values()) + spreads:
        copy.wait_send()


def gather_weights(task_weights, activations, collective_id):
    count = lax.axis_size("dp")
    inner = inner_of(count)
    outer = count // inner
    tasks, rows, cols = task_weights.shape
    _, tokens, width = activations.shape
    near, far = max(inner - 1, 1), max(outer - 1, 1)
    wide = 256 if width % 256 == 0 else width
    dma = pltpu.SemaphoreType.DMA
    vmem = pl.BlockSpec(memory_space=pltpu.VMEM)
    return pl.pallas_call(
        functools.partial(gather_kernel, count, inner, wide),
        out_shape=(
            jax.ShapeDtypeStruct((tasks, count * rows, cols), task_weights.dtype),
            jax.ShapeDtypeStruct((tasks, 1, width), jnp.float32),
        ),
        in_specs=[vmem, pl.BlockSpec(memory_space=pl.ANY)],
        out_specs=(vmem, vmem),
        scratch_shapes=[
            pltpu.VMEM((2, tokens, width), activations.dtype),
            dma((2,)),
            dma((tasks, far)),
            dma((tasks, far)),
            dma((tasks, outer, near)),
            dma((tasks, outer, near)),
        ],
        compiler_params=pltpu.CompilerParams(
            collective_id=collective_id, has_side_effects=True
        ),
    )(task_weights, activations)


def total_kernel(count, in_ref, out_ref, slots, send, receive):
    me = lax.axis_index("dp")
    others = [(me + d) % count for d in range(1, count)]
    greet(others)
    copies = []
    for d, device in enumerate(others):
        copy = remote(in_ref, slots.at[d], send.at[d], receive.at[d], device)
        copy.start()
        copies.append(copy)
    value = in_ref[...]
    for d, copy in enumerate(copies):
        copy.wait_recv()
        value = value + slots[d]
    out_ref[...] = value
    for copy in copies:
        copy.wait_send()


def total_over(part, collective_id):
    count = lax.axis_size("dp")
    dma = pltpu.SemaphoreType.DMA
    vmem = pl.BlockSpec(memory_space=pltpu.VMEM)
    return pl.pallas_call(
        functools.partial(total_kernel, count),
        out_shape=jax.ShapeDtypeStruct(part.shape, jnp.float32),
        in_specs=[vmem],
        out_specs=vmem,
        scratch_shapes=[
            pltpu.VMEM((count - 1,) + part.shape, jnp.float32),
            dma((count - 1,)),
            dma((count - 1,)),
        ],
        compiler_params=pltpu.CompilerParams(
            collective_id=collective_id, has_side_effects=True
        ),
    )(part)


def dot(left, right, dims):
    return lax.dot_general(
        left, right, (dims, ((), ())), preferred_element_type=jnp.float32
    )


def rounded(array):
    return lax.reduce_precision(array, 8, 7)


def split_pair(array):
    coarse = rounded(array)
    high = coarse.astype(jnp.bfloat16)
    low = (array - coarse).astype(jnp.bfloat16)
    return jnp.concatenate([high, low], axis=1)


def shards(activations, task_weights):
    tasks, tokens, width = activations.shape
    cols = task_weights.shape[2]
    total = tasks * tokens * lax.axis_size("dp")
    bf16, f32 = jnp.bfloat16, jnp.float32
    flat = activations.reshape(tasks * tokens, width)
    weights, squares = gather_weights(task_weights, activations, 4)
    squares = squares.reshape(tasks, width)
    squares_all = jnp.sum(squares, axis=0)[:, None]
    mean = jnp.mean(weights.astype(f32), axis=0)
    mean_pair = split_pair(mean)
    gaps = []
    for task in range(tasks):
        wide = dot(
            activations[task],
            jnp.concatenate([weights[task], mean_pair], axis=1),
            ((1,), (0,)),
        )
        outputs = rounded(wide[:, :cols])
        gaps.append(outputs - (wide[:, cols : 2 * cols] + wide[:, 2 * cols :]))
    gap = split_pair(jnp.concatenate(gaps, axis=0))
    diag = sum(
        squares[t][:, None] * (weights[t].astype(f32) - mean) for t in range(tasks)
    )
    inner = dot(flat, gap, ((0,), (0,)))
    inner = inner[:, :cols] + inner[:, cols:]
    residual, full_bf = reduce_gather(
        (ALPHA * inner + (1.0 - ALPHA) * diag) / total, f32, 1
    )
    full = full_bf.astype(f32)
    projected = dot(flat, full_bf, ((1,), (0,))).astype(bf16)
    inner = dot(flat, projected, ((0,), (0,)))
    image, image_bf = reduce_gather(
        (ALPHA * inner + (1.0 - ALPHA) * squares_all * full) / total, bf16, 2
    )
    image_full = image_bf.astype(f32)
    norm0 = jnp.sum(full * full, axis=0)
    alpha0 = norm0 / jnp.sum(full * image_full, axis=0)
    next_full = full - alpha0 * image_full
    norm1 = jnp.sum(next_full * next_full, axis=0)
    beta = norm1 / norm0
    direction = next_full + beta * full
    direction_bf = direction.astype(bf16)
    direction = direction_bf.astype(f32)
    projected = dot(flat, direction_bf, ((1,), (0,)))
    energy = (
        ALPHA * jnp.sum(projected * projected, axis=0)
        + (1.0 - ALPHA) * jnp.sum(squares_all * direction * direction, axis=0)
    ) / total
    energy = total_over(jnp.broadcast_to(energy, (8, cols)), 3)[0]
    alpha1 = norm1 / energy
    own_mean = jnp.mean(task_weights.astype(f32), axis=0)
    return (
        own_mean
        + alpha0 * residual
        + alpha1 * (residual - alpha0 * image + beta * residual)
    )


def solution(mesh):
    return jax.shard_map(
        shards,
        mesh=mesh,
        in_specs=(P(None, "dp", None), P(None, "dp", "mp")),
        out_specs=P("dp", "mp"),
        check_vma=False,
    )
```
